256 devices in a mesh: sa: 32 (over y, z), sb: 8 (over x, core).
Axes of the slice: x: 4, y: 4, z: 8, core: 2. Of those that a mesh axis runs over, the one named last changes fastest.
Arguments:
- queries: bfloat16 [131072, 4096], P(('sa', 'sb')), may hold values from -6 to 6
- keys: bfloat16 [131072, 4096], P(('sa', 'sb')), may hold values from -0.5390625 to 0.5390625
- values: bfloat16 [131072, 2048], P(('sa', 'sb')), may hold values from -6 to 6
- level_weights: bfloat16 [131072, 18, 32], P(('sa', 'sb')), may hold values from 0.25 to 4
- out_gain: bfloat16 [2048], replicated, may hold values from 0.25 to 1.75
Outputs:
- mixed: bfloat16 [131072, 2048], P(('sa', 'sb'))
The draws below stay inside these ranges and needn't reach their ends.
All inputs are finite; a program needn't handle non-finite values.
Results may differ from the reference program's by a relative error of at most 0.008.
Values sent between devices are 32-bit elements; how exact they have to be, the bound alone decides.
No kernel may reach another device: no remote copies, remote signals or barrier semaphores. Data moves between devices by JAX's collectives and lax.ppermute only.
A program may use at most 192 MiB of HBM per device.

```python
import math
import jax
import jax.numpy as jnp
from jax import lax

H = 32
DK = 128
DV = 64
TOK_DEV = 512
TOK_BITS = 9
DEV_BITS = 8
LEVELS = 18
TOKENS = 131072
N_SA = 32
N_SB = 8


def block_scale(own_key, shape, split, smallest, top_value):
    gain, own = 1.0, jax.random.fold_in(own_key, 6)
    for dim, parts in split:
        draws = jnp.exp(jax.random.uniform(jax.random.fold_in(own, dim), (parts,), jnp.float32, smallest / len(split), top_value / len(split)))
        gain = gain * jnp.repeat(draws, shape[dim] // parts).reshape([-1 if axis == dim else 1 for axis in range(len(shape))])
    return gain


def normal_values(own_key, shape, width, limit, cuts=(), held_as=jnp.bfloat16):
    values = jax.random.normal(own_key, shape, jnp.float32) * width
    if len(cuts) > 0:
        values = block_scale(own_key, shape, cuts, -0.22, 0.18) * values
    return jnp.clip(values, min=-limit, max=limit).astype(held_as)


def setup_inputs(seed: int = 0) -> dict:
    streams_of = jax.random.split(jax.random.key(seed), 6)
    return {
        "queries": normal_values(streams_of[0], (TOKENS, H * DK), 1.0, 6.0, ((0, 256),)),
        "keys": normal_values(streams_of[1], (TOKENS, H * DK), 0.09, 0.5390625, ((0, 256),)),
        "values": normal_values(streams_of[2], (TOKENS, H * DV), 1.0, 6.0, ((0, 256),)),
        "level_weights": jnp.clip(jnp.exp(math.log(4.0) - 2.7725887 * jax.random.uniform(streams_of[3], (TOKENS, LEVELS, H), jnp.float32) ** block_scale(streams_of[3], (TOKENS, LEVELS, H), ((0, 256),), -0.2, 0.2)), 0.25, 4.0).astype(jnp.bfloat16),
        "out_gain": jnp.clip(1.0 + 0.15 * jax.random.normal(streams_of[4], (H * DV,), jnp.float32), 0.25, 1.75).astype(jnp.bfloat16),
    }


epsilon = 1e-06

def block_levels(length):
    position = jnp.arange(length, dtype=jnp.int32)
    xored = jnp.bitwise_xor(position[:, None], position[None, :])
    level_index = jnp.zeros((length, length), jnp.int32)
    for level_bit in range(TOK_BITS):
        level_index = level_index + (xored >= 1 << level_bit).astype(jnp.int32)
    level_table = level_index[:, :, None] == jnp.arange(TOK_BITS + 1, dtype=jnp.int32)[None, None, :]
    causal = position[:, None] >= position[None, :]
    return (level_table & causal[:, :, None]).astype(jnp.float32)

def local_block(level_table, query_matrix_rows, key_matrix_rows, value_matrix_rows, weight_rows):
    weight = jnp.einsum('tsl,tlh->hts', level_table, weight_rows[:, :TOK_BITS + 1, :].astype(jnp.float32), precision=lax.Precision.HIGHEST)
    scores = jnp.einsum('thk,shk->hts', query_matrix_rows.astype(jnp.float32), key_matrix_rows.astype(jnp.float32), precision=lax.Precision.HIGHEST)
    weighted = (scores * weight).astype(jnp.bfloat16)
    summed = jnp.einsum('hts,shv->thv', weighted.astype(jnp.float32), value_matrix_rows.astype(jnp.float32), precision=lax.Precision.HIGHEST)
    segment_block_state = jnp.einsum('tdw,tdr->dwr', key_matrix_rows.astype(jnp.float32), value_matrix_rows.astype(jnp.float32), precision=lax.Precision.HIGHEST)
    return (summed, segment_block_state)

def normalize(summed, out_gain):
    inverse_rms = lax.rsqrt(lax.optimization_barrier(jnp.mean(summed * summed, axis=-1, keepdims=True)) + epsilon)
    gain_rows = out_gain.reshape(H, DV).astype(jnp.float32)
    return (summed * inverse_rms * gain_rows).reshape(summed.shape[0], H * DV).astype(jnp.bfloat16)

def reference(queries, keys, values, level_weights, out_gain):
    blocks = N_SA * N_SB
    query_blocks = queries.reshape(blocks, TOK_DEV, H, DK)
    key_blocks = keys.reshape(blocks, TOK_DEV, H, DK)
    value_blocks = values.reshape(blocks, TOK_DEV, H, DV)
    weight_blocks = level_weights.reshape(blocks, TOK_DEV, LEVELS, H)
    level_table = block_levels(TOK_DEV)
    local_sums, states = lax.map(lambda pieces: local_block(level_table, *pieces), (query_blocks, key_blocks, value_blocks, weight_blocks))
    level_sums = []
    current = states
    for rank_bit in range(DEV_BITS):
        level_sums.append(current)
        current = current.reshape(-1, 2, H, DK, DV).sum(1)

    def finish(pieces):
        block_index, query_matrix_rows, weight_rows, summed = pieces
        query_single_float = query_matrix_rows.astype(jnp.float32)
        for rank_bit in range(DEV_BITS):
            partner = jnp.bitwise_xor(block_index >> rank_bit, 1).astype(jnp.int32)
            fenwick_level_state = lax.dynamic_index_in_dim(level_sums[rank_bit], partner, 0, keepdims=False)
            active_flag = (block_index >> rank_bit & 1).astype(jnp.float32)
            state_readout_output = jnp.einsum('jeu,eud->jed', query_single_float, fenwick_level_state, precision=lax.Precision.HIGHEST)
            factor = weight_rows[:, TOK_BITS + 1 + rank_bit, :].astype(jnp.float32) * active_flag
            summed = summed + factor[:, :, None] * state_readout_output
        return normalize(summed, out_gain)
    block_ids = jnp.arange(blocks, dtype=jnp.int32)
    mixed = lax.map(finish, (block_ids, query_blocks, weight_blocks, local_sums))
    return mixed.reshape(TOKENS, H * DV)
```

```python
import jax
import jax.numpy as jnp
from jax import lax
from jax.experimental import pallas as pl
from jax.experimental.pallas import tpu as pltpu
from jax.sharding import Mesh, PartitionSpec as P

HEADS = 32
DK = 128
DV = 64
TOK = 512
HALF = 256
TILE = 128
LOCAL = 10
LEVELS = 18
GROUP = 4
STEPS = HEADS // GROUP
EPS = 1e-06
F32 = jnp.float32
BF16 = jnp.bfloat16


def xor_permute(value, axis, mask):
    size = lax.axis_size(axis)
    return lax.ppermute(value, axis, [(i, i ^ mask) for i in range(size)])


def dot_t0(a, b):
    return lax.dot_general(a, b, (((0,), (0,)), ((), ())), preferred_element_type=F32)


def dot_t1(a, b):
    return lax.dot_general(a, b, (((1,), (1,)), ((), ())), preferred_element_type=F32)


def state_kernel(k_ref, v_ref, s_ref, first_ref):
    for pair in range(GROUP // 2):
        v = v_ref[:, pair * 2 * DV : (pair + 1) * 2 * DV]
        k = k_ref[:, pair * 2 * DK : (pair + 1) * 2 * DK]
        first = dot_t0(v[:HALF], k[:HALF])
        both = first + dot_t0(v[HALF:], k[HALF:])
        for j in range(2):
            rows = slice(j * DV, (j + 1) * DV)
            cols = slice(j * DK, (j + 1) * DK)
            s_ref[2 * pair + j] = both[rows, cols]
            first_ref[2 * pair + j] = first[rows, cols].astype(BF16)


def block_state(keys, values):
    return pl.pallas_call(
        state_kernel,
        grid=(STEPS,),
        in_specs=[
            pl.BlockSpec((TOK, GROUP * DK), lambda i: (0, i)),
            pl.BlockSpec((TOK, GROUP * DV), lambda i: (0, i)),
        ],
        out_specs=[
            pl.BlockSpec((GROUP, DV, DK), lambda i: (i, 0, 0)),
            pl.BlockSpec((GROUP, DV, DK), lambda i: (i, 0, 0)),
        ],
        out_shape=[
            jax.ShapeDtypeStruct((HEADS, DV, DK), F32),
            jax.ShapeDtypeStruct((HEADS, DV, DK), BF16),
        ],
        cost_estimate=pl.CostEstimate(flops=2 * TOK * 4096 * 128, bytes_accessed=8 << 20, transcendentals=0),
        compiler_params=pltpu.CompilerParams(vmem_limit_bytes=24 << 20),
        name="block_state",
    )(keys, values)


def diagonal_weight(rows):
    group = lax.broadcasted_iota(jnp.int32, (16, TILE), 0)
    lane = lax.broadcasted_iota(jnp.int32, (16, TILE), 1)
    other = lane >> 3
    xored = group ^ other
    coarse = jnp.zeros((16, TILE), F32)
    for level in range(4, 8):
        coarse = jnp.where((xored >> (level - 4)) == 1, rows[level], coarse)
    coarse = jnp.where(other > group, coarse, 0.0)
    sub = lax.broadcasted_iota(jnp.int32, (8, TILE), 0)
    low = lax.broadcasted_iota(jnp.int32, (8, TILE), 1)
    place = low & 7
    near = sub ^ place
    fine = jnp.broadcast_to(rows[0], (8, TILE))
    for level in range(1, 4):
        fine = jnp.where((near >> (level - 1)) == 1, rows[level], fine)
    fine = jnp.where(place >= sub, fine, 0.0)
    owner = low >> 3
    return [
        jnp.where(owner == i, fine, jnp.broadcast_to(coarse[i : i + 1], (8, TILE)))
        for i in range(16)
    ]


def local_kernel(q_ref, k_ref, v_ref, lw_ref, first_ref, o_ref):
    for pair in range(GROUP // 2):
        v_t = v_ref[:, pair * 2 * DV : (pair + 1) * 2 * DV].T
        for j in range(2):
            head = 2 * pair + j
            cols = slice(head * DK, (head + 1) * DK)
            for block in range(2):
                at = block * HALF
                q = q_ref[at : at + HALF, cols]
                k = k_ref[at : at + HALF, cols]
                scores = dot_t1(k, q)
                tiles = []
                for tile in range(2):
                    spot = at + tile * TILE
                    rows = [lw_ref[head, l : l + 1, spot : spot + TILE] for l in range(8)]
                    weight = jnp.concatenate(diagonal_weight(rows), axis=0)
                    part = slice(tile * TILE, (tile + 1) * TILE)
                    tiles.append((scores[part, part] * weight).astype(BF16))
                across = lw_ref[head, 8:9, at + TILE : at + HALF]
                upper = (scores[:TILE, TILE:] * across).astype(BF16)
                zero = jnp.zeros((TILE, TILE), BF16)
                weighted = jnp.concatenate(
                    [
                        jnp.concatenate([tiles[0], upper], axis=1),
                        jnp.concatenate([zero, tiles[1]], axis=1),
                    ],
                    axis=0,
                )
                v_part = v_t[j * DV : (j + 1) * DV, at : at + HALF]
                out = jnp.dot(v_part, weighted, preferred_element_type=F32)
                if block == 1:
                    out = out + lw_ref[head, 9:10, at : at + HALF] * dot_t1(first_ref[head], q)
                o_ref[head, :, at : at + HALF] = out


def local_attention(queries, keys, values, rows, first):
    return pl.pallas_call(
        local_kernel,
        grid=(STEPS,),
        in_specs=[
            pl.BlockSpec((TOK, GROUP * DK), lambda i: (0, i)),
            pl.BlockSpec((TOK, GROUP * DK), lambda i: (0, i)),
            pl.BlockSpec((TOK, GROUP * DV), lambda i: (0, i)),
            pl.BlockSpec((GROUP, LEVELS, TOK), lambda i: (i, 0, 0)),
            pl.BlockSpec((GROUP, DV, DK), lambda i: (i, 0, 0)),
        ],
        out_specs=pl.BlockSpec((GROUP, DV, TOK), lambda i: (i, 0, 0)),
        out_shape=jax.ShapeDtypeStruct((HEADS, DV, TOK), F32),
        cost_estimate=pl.CostEstimate(flops=8 << 30, bytes_accessed=16 << 20, transcendentals=0),
        compiler_params=pltpu.CompilerParams(vmem_limit_bytes=24 << 20),
        name="local_attention",
    )(queries, keys, values, rows, first)


def finish_kernel(
    place_ref, q_ref, local_ref, lw_ref, gain_ref, zero_ref,
    own1_ref, oth1_ref, own2_ref, oth2_ref, own3_ref, oth3_ref, o_ref, lhs_ref,
):
    step = pl.program_id(0)

    def stage(a, b, c):
        for j in range(GROUP):
            lhs_ref[j, 64:128] = a[0, 0, j].astype(BF16)
            lhs_ref[j, 128:192] = a[0, 1, j].astype(BF16)
            lhs_ref[j, 192:384] = b[0, j].astype(BF16)
            lhs_ref[j, 384:512] = c[0, j].astype(BF16)

    for j in range(GROUP):
        lhs_ref[j, 0:64] = zero_ref[j].astype(BF16)

    @pl.when(step < STEPS // 2)
    def _():
        stage(own1_ref, own2_ref, own3_ref)

    @pl.when(step >= STEPS // 2)
    def _():
        stage(oth1_ref, oth2_ref, oth3_ref)

    for pair in range(GROUP // 2):
        for block in range(2):
            at = slice(block * HALF, (block + 1) * HALF)
            outs = []
            for j in range(2):
                head = 2 * pair + j
                q = q_ref[at, head * DK : (head + 1) * DK]
                r = dot_t1(lhs_ref[head], q)
                w = [lw_ref[head, LOCAL + l : LOCAL + l + 1, at] for l in range(8)]
                acc = local_ref[head, :, at] + r[0:64] * w[0] + r[64:128] * w[1] + r[128:192] * w[2]
                halves = []
                for half in range(2):
                    part = acc[half * 32 : (half + 1) * 32]
                    for l in range(3):
                        base = 192 + half * 96 + l * 32
                        part = part + r[base : base + 32] * w[3 + l]
                    for l in range(2):
                        base = 384 + half * 64 + l * 32
                        part = part + r[base : base + 32] * w[6 + l]
                    halves.append(part)
                acc = jnp.concatenate(halves, axis=0)
                mean = jnp.mean(acc * acc, axis=0, keepdims=True)
                outs.append(acc * lax.rsqrt(mean + EPS))
            flat = jnp.concatenate(outs, axis=0).T
            cols = slice(pair * 2 * DV, (pair + 1) * 2 * DV)
            o_ref[at, cols] = (flat * gain_ref[:, cols]).astype(BF16)


def finish(place, queries, local, rows, gain, zero, own, oth):
    def group(i, place):
        return 4 * (place[0] ^ (i // 4)) + (place[1] ^ (i % 4))

    def own_index(i):
        return jnp.minimum(i, 3)

    def oth_index(i):
        return jnp.maximum(i - 4, 0)

    def pieces(array, index):
        block = (1,) + array.shape[1:]
        rank = len(block)
        return pl.BlockSpec(block, lambda i, place: (index(i),) + (0,) * (rank - 1))

    sides = []
    specs = []
    for mine, theirs in zip(own, oth):
        sides += [mine, theirs]
        specs += [pieces(mine, own_index), pieces(theirs, oth_index)]
    return pl.pallas_call(
        finish_kernel,
        grid_spec=pltpu.PrefetchScalarGridSpec(
            num_scalar_prefetch=1,
            grid=(STEPS,),
            in_specs=[
                pl.BlockSpec((TOK, GROUP * DK), lambda i, p: (0, group(i, p))),
                pl.BlockSpec((GROUP, DV, TOK), lambda i, p: (group(i, p), 0, 0)),
                pl.BlockSpec((GROUP, LEVELS, TOK), lambda i, p: (group(i, p), 0, 0)),
                pl.BlockSpec((1, GROUP * DV), lambda i, p: (0, group(i, p))),
                pl.BlockSpec((GROUP, DV, DK), lambda i, p: (group(i, p), 0, 0)),
            ]
            + specs,
            out_specs=pl.BlockSpec((TOK, GROUP * DV), lambda i, p: (0, group(i, p))),
            scratch_shapes=[pltpu.VMEM((GROUP, 8 * DV, DK), BF16)],
        ),
        out_shape=jax.ShapeDtypeStruct((TOK, HEADS * DV), BF16),
        cost_estimate=pl.CostEstimate(flops=9 << 30, bytes_accessed=20 << 20, transcendentals=0),
        compiler_params=pltpu.CompilerParams(vmem_limit_bytes=32 << 20),
        name="finish",
    )(place, queries, local, rows, gain, zero, *sides)


def gathered(payload):
    return jnp.stack([payload[0]] + [xor_permute(payload[d], "x", d) for d in range(1, 4)])


def on_device(queries, keys, values, level_weights, out_gain):
    core, x, z, y = (lax.axis_index(a) for a in ("c", "x", "z", "y"))
    block = ((y * 8 + z) * 4 + x) * 2 + core
    state, first = block_state(keys, values)

    scale = [1.0] * LOCAL + [(block >> j & 1).astype(F32) for j in range(8)]
    scale = jnp.stack([jnp.asarray(s, F32) for s in scale])
    rows = jnp.transpose(level_weights, (2, 1, 0)).astype(F32) * scale[None, :, None]

    local = local_attention(queries, keys, values, rows, first)

    partner = xor_permute(state, "c", 1)
    half = lax.dynamic_slice_in_dim(state, core * 16, 16, 0) + lax.dynamic_slice_in_dim(
        partner, core * 16, 16, 0
    )
    u = lax.all_to_all(half.reshape(4, GROUP * DV, DK), "x", 0, 0, tiled=True)
    pairs = u[0::2] + u[1::2]
    row_sum = pairs[0] + pairs[1]
    low = []
    for d in range(4):
        to = x ^ d
        one = lax.dynamic_index_in_dim(u, to ^ 1, 0, keepdims=False)
        two = lax.dynamic_index_in_dim(pairs, (to >> 1) ^ 1, 0, keepdims=False)
        low.append(jnp.stack([one, two]).reshape(2, GROUP, DV, DK))
    own1 = gathered(low)
    w = lax.all_to_all(row_sum.reshape(8, 32, DK), "z", 0, 0, tiled=True)
    w2 = w.reshape(4, 2, 32, DK)
    t4 = w2[:, 0] + w2[:, 1]
    t5 = t4[0::2] + t4[1::2]
    t6 = t5[0] + t5[1]
    p1 = xor_permute(t6, "y", 1)
    p2 = xor_permute(t6, "y", 2)
    p3 = xor_permute(t6, "y", 3)
    l3 = w2[:, ::-1].reshape(8, 32, DK)
    l4 = jnp.broadcast_to(t4.reshape(2, 2, 1, 32, DK)[:, ::-1], (2, 2, 2, 32, DK)).reshape(8, 32, DK)
    l5 = jnp.broadcast_to(t5.reshape(2, 1, 32, DK)[::-1], (2, 4, 32, DK)).reshape(8, 32, DK)
    mid = lax.all_to_all(jnp.stack([l3, l4, l5], axis=1), "z", 0, 0, tiled=True)
    top = jnp.broadcast_to(jnp.stack([p1, p2 + p3])[None], (8, 2, 32, DK))
    top = lax.all_to_all(top, "z", 0, 0, tiled=True)
    mid = mid.reshape(GROUP, 6 * 32, DK)
    top = top.reshape(GROUP, 4 * 32, DK)
    own2 = gathered([mid] * 4)
    own3 = gathered([top] * 4)
    own = [own1, own2, own3]
    oth = [xor_permute(o, "c", 1) for o in own]
    place = jnp.stack([core, x]).astype(jnp.int32)
    gain = out_gain.astype(F32).reshape(1, HEADS * DV)
    return finish(place, queries, local, rows, gain, partner, own, oth)


def solution(mesh):
    wide = Mesh(mesh.devices.reshape(4, 8, 4, 2), ("y", "z", "x", "c"))
    split = ("y", "z", "x", "c")
    return jax.shard_map(
        on_device,
        mesh=wide,
        in_specs=(P(split, None), P(split, None), P(split, None), P(split, None, None), P()),
        out_specs=P(split, None),
        check_vma=False,
    )
```

```python
import functools

import jax
import jax.numpy as jnp
from jax import lax
from jax.experimental import pallas as pl
from jax.experimental.pallas import tpu as pltpu
from jax.sharding import Mesh, PartitionSpec as P

HEADS = 32
DK = 128
DV = 64
TOK = 512
HALF = 256
TILE = 128
LOCAL = 10
LEVELS = 18
GROUP = 4
STEPS = HEADS // GROUP
SIDE = HEADS // 2
EPS = 1e-06
F32 = jnp.float32
BF16 = jnp.bfloat16


def xor_permute(value, axis, mask):
    size = lax.axis_size(axis)
    return lax.ppermute(value, axis, [(i, i ^ mask) for i in range(size)])


def dot(a, b):
    return jnp.dot(a, b, preferred_element_type=F32)


def dot_t0(a, b):
    return lax.dot_general(a, b, (((0,), (0,)), ((), ())), preferred_element_type=F32)


def dot_t1(a, b):
    return lax.dot_general(a, b, (((1,), (1,)), ((), ())), preferred_element_type=F32)


def state_kernel(other, place_ref, k_hbm, v_hbm, s_hbm, k_buf, v_buf, s_buf, k_sem, v_sem, s_sem):
    side = place_ref[0] ^ other
    chunks = SIDE // GROUP

    def copies(i):
        at = side * chunks + i
        k_at = pl.ds(pl.multiple_of(at * GROUP * DK, GROUP * DK), GROUP * DK)
        v_at = pl.ds(pl.multiple_of(at * GROUP * DV, GROUP * DV), GROUP * DV)
        return (
            pltpu.make_async_copy(k_hbm.at[:, k_at], k_buf.at[i], k_sem.at[i]),
            pltpu.make_async_copy(v_hbm.at[:, v_at], v_buf.at[i], v_sem.at[i]),
        )

    def back(i):
        heads = pl.ds(i * GROUP, GROUP)
        return pltpu.make_async_copy(s_buf.at[heads], s_hbm.at[heads], s_sem.at[i])

    for i in range(chunks):
        for copy in copies(i):
            copy.start()
    for i in range(chunks):
        for copy in copies(i):
            copy.wait()
        for pair in range(GROUP // 2):
            v = v_buf[i, :, pair * 2 * DV : (pair + 1) * 2 * DV]
            k = k_buf[i, :, pair * 2 * DK : (pair + 1) * 2 * DK]
            both = dot_t0(v, k)
            for j in range(2):
                s_buf[i * GROUP + 2 * pair + j] = both[j * DV : (j + 1) * DV, j * DK : (j + 1) * DK]
        back(i).start()
    for i in range(chunks):
        back(i).wait()


def block_state(place, keys, values, other):
    hbm = pl.BlockSpec(memory_space=pl.ANY)
    chunks = SIDE // GROUP
    return pl.pallas_call(
        functools.partial(state_kernel, other),
        in_specs=[pl.BlockSpec(memory_space=pltpu.SMEM), hbm, hbm],
        out_specs=hbm,
        out_shape=jax.ShapeDtypeStruct((SIDE, DV, DK), F32),
        scratch_shapes=[
            pltpu.VMEM((chunks, TOK, GROUP * DK), BF16),
            pltpu.VMEM((chunks, TOK, GROUP * DV), BF16),
            pltpu.VMEM((SIDE, DV, DK), F32),
            pltpu.SemaphoreType.DMA((chunks,)),
            pltpu.SemaphoreType.DMA((chunks,)),
            pltpu.SemaphoreType.DMA((chunks,)),
        ],
        cost_estimate=pl.CostEstimate(flops=1 << 28, bytes_accessed=4 << 20, transcendentals=0),
        compiler_params=pltpu.CompilerParams(vmem_limit_bytes=60 << 20),
        name="block_state",
    )(place, keys, values)


def diagonal_weight(rows):
    group = lax.broadcasted_iota(jnp.int32, (16, TILE), 0)
    lane = lax.broadcasted_iota(jnp.int32, (16, TILE), 1)
    other = lane >> 3
    xored = group ^ other
    coarse = jnp.zeros((16, TILE), F32)
    for level in range(4, 8):
        coarse = jnp.where((xored >> (level - 4)) == 1, rows[level], coarse)
    coarse = jnp.where(other > group, coarse, 0.0)
    sub = lax.broadcasted_iota(jnp.int32, (8, TILE), 0)
    low = lax.broadcasted_iota(jnp.int32, (8, TILE), 1)
    place = low & 7
    near = sub ^ place
    fine = jnp.broadcast_to(rows[0], (8, TILE))
    for level in range(1, 4):
        fine = jnp.where((near >> (level - 1)) == 1, rows[level], fine)
    fine = jnp.where(place >= sub, fine, 0.0)
    owner = low >> 3
    return jnp.concatenate(
        [
            jnp.where(owner == i, fine, jnp.broadcast_to(coarse[i : i + 1], (8, TILE)))
            for i in range(16)
        ],
        axis=0,
    )


def local_kernel(place_ref, q_ref, k_ref, v_ref, lw_ref, o_ref, w_ref):
    step = pl.program_id(0)

    for r in range(SIDE // GROUP):

        @pl.when(step % 4 == r)
        def _():
            w_ref[...] = lw_ref[:LOCAL, r * GROUP : (r + 1) * GROUP].astype(F32)

    def row(level, head, at, size):
        return w_ref[level, head : head + 1, at : at + size]

    v_t = [v_ref[:, p * 2 * DV : (p + 1) * 2 * DV].T for p in range(GROUP // 2)]
    parts = {}
    for head in range(GROUP):
        cols = slice(head * DK, (head + 1) * DK)
        v_head = v_t[head // 2][(head % 2) * DV : (head % 2 + 1) * DV]
        for block in range(2):
            at = block * HALF
            q = q_ref[at : at + HALF, cols]
            k = k_ref[at : at + HALF, cols]
            if block:
                first = dot(v_head[:, :HALF], k_ref[:HALF, cols]).astype(BF16)
                scores = dot_t1(jnp.concatenate([k, first], axis=0), q)
                extra = scores[HALF:] * row(9, head, at, HALF)
            else:
                scores = dot_t1(k, q)
                extra = None
            tiles = []
            for tile in range(2):
                part = slice(tile * TILE, (tile + 1) * TILE)
                rows = [row(l, head, at + tile * TILE, TILE) for l in range(8)]
                tiles.append((scores[part, part] * diagonal_weight(rows)).astype(BF16))
            upper = (scores[:TILE, TILE:HALF] * row(8, head, at + TILE, TILE)).astype(BF16)
            weighted = jnp.concatenate(
                [
                    jnp.concatenate([tiles[0], upper], axis=1),
                    jnp.concatenate([jnp.zeros((TILE, TILE), BF16), tiles[1]], axis=1),
                ],
                axis=0,
            )
            parts[head, block] = (v_head[:, at : at + HALF], weighted, extra)
    for (head, block), (v_part, weighted, extra) in parts.items():
        out = dot(v_part, weighted)
        o_ref[head, :, block * HALF : (block + 1) * HALF] = out if extra is None else out + extra


def local_attention(place, queries, keys, values, level_rows):
    return pl.pallas_call(
        local_kernel,
        grid_spec=pltpu.PrefetchScalarGridSpec(
            num_scalar_prefetch=1,
            grid=(STEPS,),
            in_specs=[
                pl.BlockSpec((TOK, GROUP * DK), lambda i, p: (0, i)),
                pl.BlockSpec((TOK, GROUP * DK), lambda i, p: (0, i)),
                pl.BlockSpec((TOK, GROUP * DV), lambda i, p: (0, i)),
                pl.BlockSpec((LEVELS, SIDE, TOK), lambda i, p: (0, i // 4, 0)),
            ],
            out_specs=pl.BlockSpec((GROUP, DV, TOK), lambda i, p: (i, 0, 0)),
            scratch_shapes=[pltpu.VMEM((LOCAL, GROUP, TOK), F32)],
        ),
        out_shape=jax.ShapeDtypeStruct((HEADS, DV, TOK), F32),
        cost_estimate=pl.CostEstimate(flops=8 << 30, bytes_accessed=16 << 20, transcendentals=0),
        compiler_params=pltpu.CompilerParams(vmem_limit_bytes=60 << 20),
        name="local_attention",
    )(place, queries, keys, values, level_rows)


def readout_kernel(base, counts, last, *refs):
    refs = list(refs)
    place_ref, q_ref, sum_ref, lw_ref = refs[:4]
    refs = refs[4:]
    gain_ref = refs.pop(0) if last else None
    sides = [(refs[2 * i], refs[2 * i + 1]) for i in range(len(counts))]
    o_ref, lhs_ref, w_ref = refs[-3:]
    step = pl.program_id(0)
    levels = sum(counts)

    for r in range(SIDE // GROUP):

        @pl.when(step % 4 == r)
        def _():
            for l in range(levels):
                flag = ((place_ref[2] >> (base + l)) & 1).astype(F32)
                rows = lw_ref[LOCAL + base + l, r * GROUP : (r + 1) * GROUP]
                w_ref[l] = rows.astype(F32) * flag

    def stage(which):
        at = 0
        for pair, count in zip(sides, counts):
            for level in range(count):
                for j in range(GROUP):
                    lhs_ref[j, at : at + DV] = pair[which][0, level, j].astype(BF16)
                at += DV

    @pl.when(step < STEPS // 2)
    def _():
        stage(0)

    @pl.when(step >= STEPS // 2)
    def _():
        stage(1)

    for pair in range(GROUP // 2):
        for block in range(2):
            at = slice(block * HALF, (block + 1) * HALF)
            outs = []
            for j in range(2):
                head = 2 * pair + j
                q = q_ref[at, head * DK : (head + 1) * DK]
                r = dot_t1(lhs_ref[head], q)
                acc = sum_ref[head, :, at]
                for l in range(levels):
                    weight = w_ref[l, head : head + 1, at]
                    acc = acc + r[l * DV : (l + 1) * DV] * weight
                if last:
                    mean = jnp.mean(acc * acc, axis=0, keepdims=True)
                    outs.append(acc * lax.rsqrt(mean + EPS))
                else:
                    o_ref[head, :, at] = acc
            if last:
                flat = jnp.concatenate(outs, axis=0).T
                cols = slice(pair * 2 * DV, (pair + 1) * 2 * DV)
                o_ref[at, cols] = (flat * gain_ref[:, cols]).astype(BF16)


def readout(place, queries, total, level_rows, base, own, oth, distance, gain=None):
    last = gain is not None
    counts = tuple(o.shape[1] for o in own)
    levels = sum(counts)

    def group(i, place):
        return 4 * (place[0] ^ (i // 4)) + i % 4

    def pieces(array, second, by_distance):
        def index(i, place):
            at = jnp.maximum(i - 4, 0) if second else jnp.minimum(i, 3)
            return (at ^ place[1] if by_distance else at, 0, 0, 0, 0)

        return pl.BlockSpec((1,) + array.shape[1:], index)

    heads = pl.BlockSpec((GROUP, DV, TOK), lambda i, p: (group(i, p), 0, 0))
    flat = pl.BlockSpec((TOK, GROUP * DV), lambda i, p: (0, group(i, p)))
    args = [queries, total, level_rows]
    specs = [
        pl.BlockSpec((TOK, GROUP * DK), lambda i, p: (0, group(i, p))),
        heads,
        pl.BlockSpec((LEVELS, SIDE, TOK), lambda i, p: (0, p[0] ^ (i // 4), 0)),
    ]
    if last:
        args.append(gain)
        specs.append(pl.BlockSpec((1, GROUP * DV), lambda i, p: (0, group(i, p))))
    for mine, theirs, by_distance in zip(own, oth, distance):
        args += [mine, theirs]
        specs += [pieces(mine, False, by_distance), pieces(theirs, True, by_distance)]
    return pl.pallas_call(
        functools.partial(readout_kernel, base, counts, last),
        grid_spec=pltpu.PrefetchScalarGridSpec(
            num_scalar_prefetch=1,
            grid=(STEPS,),
            in_specs=specs,
            out_specs=flat if last else heads,
            scratch_shapes=[
                pltpu.VMEM((GROUP, levels * DV, DK), BF16),
                pltpu.VMEM((levels, GROUP, TOK), F32),
            ],
        ),
        out_shape=jax.ShapeDtypeStruct((TOK, HEADS * DV), BF16)
        if last
        else jax.ShapeDtypeStruct((HEADS, DV, TOK), F32),
        cost_estimate=pl.CostEstimate(flops=levels << 30, bytes_accessed=16 << 20, transcendentals=0),
        compiler_params=pltpu.CompilerParams(vmem_limit_bytes=24 << 20),
        name="readout_last" if last else "readout",
    )(place, *args)


def after(value, *others):
    return lax.optimization_barrier((value, *others))[0]


def row_exchange(payload):
    return lax.all_to_all(payload, "x", 0, 0, tiled=True)


def to_row(*levels):
    return row_exchange(jnp.broadcast_to(jnp.stack(levels)[None], (4, len(levels)) + levels[0].shape))


def sent(payload):
    return [payload] + [xor_permute(payload, "x", d) for d in range(1, 4)]


def on_device(queries, keys, values, level_weights, out_gain):
    core, x, z, y = (lax.axis_index(a) for a in ("c", "x", "z", "y"))
    block = ((y * 8 + z) * 4 + x) * 2 + core
    place = jnp.stack([core, x, block]).astype(jnp.int32)
    level_rows = jnp.transpose(level_weights, (1, 2, 0))
    gain = out_gain.astype(F32).reshape(1, HEADS * DV)

    give = block_state(place, keys, values, 1)
    zero_own = xor_permute(give, "c", 1)
    keep = block_state(after(place, give), keys, values, 0)
    half = keep + zero_own
    u = row_exchange(half.reshape(4, GROUP, DV, DK))
    zero_oth = xor_permute(after(keep, half), "c", 1)
    local = local_attention(after(place, half), queries, keys, values, level_rows)
    u, local = lax.optimization_barrier((u, local))
    t3 = (u[0] + u[1]) + (u[2] + u[3])
    l3 = xor_permute(t3, "z", 1)
    l1 = xor_permute(after(half, u), "x", 1)
    t4 = t3 + l3
    l4 = xor_permute(t4, "z", 2)
    t5 = after(t4 + l4, l1)
    l2 = xor_permute(half + l1, "x", 3)
    l5 = xor_permute(t5, "z", 4)
    own34 = to_row(l3, l4)
    t6 = t5 + l5
    p1, p2, p3 = (xor_permute(t6, "y", d) for d in (1, 2, 3))
    p1 = after(p1, l2)
    top = jnp.stack([l5, p1, p2 + p3])
    own567 = sent(top)
    early = [part.reshape(4, 1, GROUP, DV, DK) for part in (after(l1, t5), after(l2, top))]
    own = [zero_own.reshape(4, 1, GROUP, DV, DK)] + early
    oth = [zero_oth.reshape(4, 1, GROUP, DV, DK)] + [xor_permute(part, "c", 1) for part in early]
    own34 = after(own34, top)
    own.append(own34)
    oth.append(xor_permute(own34, "c", 1))
    mid = readout(place, queries, local, level_rows, 0, own, oth, [False] * 4)
    own567 = jnp.stack([after(part, mid) for part in own567])
    oth567 = xor_permute(own567, "c", 1)
    return readout(place, queries, mid, level_rows, 5, [own567], [oth567], [True], gain=gain)


def solution(mesh):
    wide = Mesh(mesh.devices.reshape(4, 8, 4, 2), ("y", "z", "x", "c"))
    split = ("y", "z", "x", "c")
    return jax.shard_map(
        on_device,
        mesh=wide,
        in_specs=(P(split, None), P(split, None), P(split, None), P(split, None, None), P()),
        out_specs=P(split, None),
        check_vma=False,
    )
```

```python
import functools

import jax
import jax.numpy as jnp
from jax import lax
from jax.experimental import pallas as pl
from jax.experimental.pallas import tpu as pltpu
from jax.sharding import Mesh, PartitionSpec as P

HEADS = 32
DK = 128
DV = 64
TOK = 512
HALF = 256
TILE = 128
LOCAL = 10
LEVELS = 18
GROUP = 4
STEPS = HEADS // GROUP
SIDE = HEADS // 2
EPS = 1e-06
F32 = jnp.float32
BF16 = jnp.bfloat16


def xor_permute(value, axis, mask):
    size = lax.axis_size(axis)
    return lax.ppermute(value, axis, [(i, i ^ mask) for i in range(size)])


def dot(a, b):
    return jnp.dot(a, b, preferred_element_type=F32)


def dot_t0(a, b):
    return lax.dot_general(a, b, (((0,), (0,)), ((), ())), preferred_element_type=F32)


def dot_t1(a, b):
    return lax.dot_general(a, b, (((1,), (1,)), ((), ())), preferred_element_type=F32)


def state_kernel(other, place_ref, k_hbm, v_hbm, s_ref, k_buf, v_buf, k_sem, v_sem):
    side = place_ref[0] ^ other
    chunks = SIDE // GROUP

    def copies(i):
        at = side * chunks + i
        k_at = pl.ds(pl.multiple_of(at * GROUP * DK, GROUP * DK), GROUP * DK)
        v_at = pl.ds(pl.multiple_of(at * GROUP * DV, GROUP * DV), GROUP * DV)
        return (
            pltpu.make_async_copy(k_hbm.at[:, k_at], k_buf.at[i], k_sem.at[i]),
            pltpu.make_async_copy(v_hbm.at[:, v_at], v_buf.at[i], v_sem.at[i]),
        )

    for i in range(chunks):
        for copy in copies(i):
            copy.start()
    for i in range(chunks):
        for copy in copies(i):
            copy.wait()
        for pair in range(GROUP // 2):
            v = v_buf[i, :, pair * 2 * DV : (pair + 1) * 2 * DV]
            k = k_buf[i, :, pair * 2 * DK : (pair + 1) * 2 * DK]
            both = dot_t0(v, k)
            for j in range(2):
                s_ref[i * GROUP + 2 * pair + j] = both[j * DV : (j + 1) * DV, j * DK : (j + 1) * DK]


def block_state(place, keys, values, other):
    hbm = pl.BlockSpec(memory_space=pltpu.HBM)
    chunks = SIDE // GROUP
    return pl.pallas_call(
        functools.partial(state_kernel, other),
        in_specs=[pl.BlockSpec(memory_space=pltpu.SMEM), hbm, hbm],
        out_specs=pl.BlockSpec(memory_space=pltpu.VMEM),
        out_shape=jax.ShapeDtypeStruct((SIDE, DV, DK), F32),
        scratch_shapes=[
            pltpu.VMEM((chunks, TOK, GROUP * DK), BF16),
            pltpu.VMEM((chunks, TOK, GROUP * DV), BF16),
            pltpu.SemaphoreType.DMA((chunks,)),
            pltpu.SemaphoreType.DMA((chunks,)),
        ],
        cost_estimate=pl.CostEstimate(flops=1 << 28, bytes_accessed=4 << 20, transcendentals=0),
        compiler_params=pltpu.CompilerParams(vmem_limit_bytes=16 << 20),
        name="block_state",
    )(place, keys, values)


def diagonal_weight(rows):
    group = lax.broadcasted_iota(jnp.int32, (16, TILE), 0)
    lane = lax.broadcasted_iota(jnp.int32, (16, TILE), 1)
    other = lane >> 3
    xored = group ^ other
    coarse = jnp.zeros((16, TILE), F32)
    for level in range(4, 8):
        coarse = jnp.where((xored >> (level - 4)) == 1, rows[level], coarse)
    coarse = jnp.where(other > group, coarse, 0.0)
    sub = lax.broadcasted_iota(jnp.int32, (8, TILE), 0)
    low = lax.broadcasted_iota(jnp.int32, (8, TILE), 1)
    place = low & 7
    near = sub ^ place
    fine = jnp.broadcast_to(rows[0], (8, TILE))
    for level in range(1, 4):
        fine = jnp.where((near >> (level - 1)) == 1, rows[level], fine)
    fine = jnp.where(place >= sub, fine, 0.0)
    owner = low >> 3
    return jnp.concatenate(
        [
            jnp.where(owner == i, fine, jnp.broadcast_to(coarse[i : i + 1], (8, TILE)))
            for i in range(16)
        ],
        axis=0,
    )


def local_kernel(place_ref, q_ref, k_ref, v_ref, lw_ref, o_ref, w_ref):
    step = pl.program_id(0)

    for r in range(SIDE // GROUP):

        @pl.when(step % 4 == r)
        def _():
            w_ref[...] = lw_ref[:LOCAL, r * GROUP : (r + 1) * GROUP].astype(F32)

    def row(level, head, at, size):
        return w_ref[level, head : head + 1, at : at + size]

    v_t = [v_ref[:, p * 2 * DV : (p + 1) * 2 * DV].T for p in range(GROUP // 2)]
    parts = {}
    for head in range(GROUP):
        cols = slice(head * DK, (head + 1) * DK)
        v_head = v_t[head // 2][(head % 2) * DV : (head % 2 + 1) * DV]
        for block in range(2):
            at = block * HALF
            q = q_ref[at : at + HALF, cols]
            k = k_ref[at : at + HALF, cols]
            if block:
                first = dot(v_head[:, :HALF], k_ref[:HALF, cols]).astype(BF16)
                scores = dot_t1(jnp.concatenate([k, first], axis=0), q)
                extra = scores[HALF:] * row(9, head, at, HALF)
            else:
                scores = dot_t1(k, q)
                extra = None
            tiles = []
            for tile in range(2):
                part = slice(tile * TILE, (tile + 1) * TILE)
                rows = [row(l, head, at + tile * TILE, TILE) for l in range(8)]
                tiles.append((scores[part, part] * diagonal_weight(rows)).astype(BF16))
            upper = (scores[:TILE, TILE:HALF] * row(8, head, at + TILE, TILE)).astype(BF16)
            weighted = jnp.concatenate(
                [
                    jnp.concatenate([tiles[0], upper], axis=1),
                    jnp.concatenate([jnp.zeros((TILE, TILE), BF16), tiles[1]], axis=1),
                ],
                axis=0,
            )
            parts[head, block] = (v_head[:, at : at + HALF], weighted, extra)
    for (head, block), (v_part, weighted, extra) in parts.items():
        out = dot(v_part, weighted)
        out = out if extra is None else out + extra
        o_ref[head, :, block * HALF : (block + 1) * HALF] = out.astype(BF16)


def local_attention(place, queries, keys, values, level_rows):
    return pl.pallas_call(
        local_kernel,
        grid_spec=pltpu.PrefetchScalarGridSpec(
            num_scalar_prefetch=1,
            grid=(STEPS,),
            in_specs=[
                pl.BlockSpec((TOK, GROUP * DK), lambda i, p: (0, i)),
                pl.BlockSpec((TOK, GROUP * DK), lambda i, p: (0, i)),
                pl.BlockSpec((TOK, GROUP * DV), lambda i, p: (0, i)),
                pl.BlockSpec((LEVELS, SIDE, TOK), lambda i, p: (0, i // 4, 0)),
            ],
            out_specs=pl.BlockSpec((GROUP, DV, TOK), lambda i, p: (i, 0, 0)),
            scratch_shapes=[pltpu.VMEM((LOCAL, GROUP, TOK), F32)],
        ),
        out_shape=jax.ShapeDtypeStruct((HEADS, DV, TOK), BF16),
        cost_estimate=pl.CostEstimate(flops=8 << 30, bytes_accessed=16 << 20, transcendentals=0),
        compiler_params=pltpu.CompilerParams(vmem_limit_bytes=60 << 20),
        name="local_attention",
    )(place, queries, keys, values, level_rows)


def readout_kernel(base, counts, last, *refs):
    refs = list(refs)
    place_ref, q_ref, sum_ref, lw_ref = refs[:4]
    refs = refs[4:]
    gain_ref = refs.pop(0) if last else None
    sides = [(refs[2 * i], refs[2 * i + 1]) for i in range(len(counts))]
    o_ref, lhs_ref, w_ref = refs[-3:]
    step = pl.program_id(0)
    levels = sum(counts)

    for r in range(SIDE // GROUP):

        @pl.when(step % 4 == r)
        def _():
            for l in range(levels):
                flag = ((place_ref[2] >> (base + l)) & 1).astype(F32)
                rows = lw_ref[LOCAL + base + l, r * GROUP : (r + 1) * GROUP]
                w_ref[l] = rows.astype(F32) * flag

    def stage(which):
        at = 0
        for pair, count in zip(sides, counts):
            for level in range(count):
                for j in range(GROUP):
                    lhs_ref[j, at : at + DV] = pair[which][0, level, j].astype(BF16)
                at += DV

    @pl.when(step < STEPS // 2)
    def _():
        stage(0)

    @pl.when(step >= STEPS // 2)
    def _():
        stage(1)

    sums = {}
    for head in range(GROUP):
        for block in range(2):
            at = slice(block * HALF, (block + 1) * HALF)
            r = dot_t1(lhs_ref[head], q_ref[at, head * DK : (head + 1) * DK])
            acc = sum_ref[head, :, at].astype(F32)
            for l in range(levels):
                acc = acc + r[l * DV : (l + 1) * DV] * w_ref[l, head : head + 1, at]
            if last:
                mean = jnp.mean(acc * acc, axis=0, keepdims=True)
                sums[head, block] = acc * lax.rsqrt(mean + EPS)
            else:
                o_ref[head, :, at] = acc
    if last:
        for pair in range(GROUP // 2):
            cols = slice(pair * 2 * DV, (pair + 1) * 2 * DV)
            for block in range(2):
                flat = jnp.concatenate([sums[2 * pair, block], sums[2 * pair + 1, block]], axis=0).T
                at = slice(block * HALF, (block + 1) * HALF)
                o_ref[at, cols] = (flat * gain_ref[:, cols]).astype(BF16)


def readout(place, queries, total, level_rows, base, own, oth, distance, gain=None):
    last = gain is not None
    counts = tuple(o.shape[1] for o in own)
    levels = sum(counts)

    def group(i, place):
        return 4 * (place[0] ^ (i // 4)) + i % 4

    def pieces(array, second, by_distance):
        def index(i, place):
            at = jnp.maximum(i - 4, 0) if second else jnp.minimum(i, 3)
            return (at ^ place[1] if by_distance else at, 0, 0, 0, 0)

        return pl.BlockSpec((1,) + array.shape[1:], index)

    heads = pl.BlockSpec((GROUP, DV, TOK), lambda i, p: (group(i, p), 0, 0))
    flat = pl.BlockSpec((TOK, GROUP * DV), lambda i, p: (0, group(i, p)))
    args = [queries, total, level_rows]
    specs = [
        pl.BlockSpec((TOK, GROUP * DK), lambda i, p: (0, group(i, p))),
        heads,
        pl.BlockSpec((LEVELS, SIDE, TOK), lambda i, p: (0, p[0] ^ (i // 4), 0)),
    ]
    if last:
        args.append(gain)
        specs.append(pl.BlockSpec((1, GROUP * DV), lambda i, p: (0, group(i, p))))
    for mine, theirs, by_distance in zip(own, oth, distance):
        args += [mine, theirs]
        specs += [pieces(mine, False, by_distance), pieces(theirs, True, by_distance)]
    return pl.pallas_call(
        functools.partial(readout_kernel, base, counts, last),
        grid_spec=pltpu.PrefetchScalarGridSpec(
            num_scalar_prefetch=1,
            grid=(STEPS,),
            in_specs=specs,
            out_specs=flat if last else heads,
            scratch_shapes=[
                pltpu.VMEM((GROUP, levels * DV, DK), BF16),
                pltpu.VMEM((levels, GROUP, TOK), F32),
            ],
        ),
        out_shape=jax.ShapeDtypeStruct((TOK, HEADS * DV), BF16)
        if last
        else jax.ShapeDtypeStruct((HEADS, DV, TOK), F32),
        cost_estimate=pl.CostEstimate(flops=levels << 30, bytes_accessed=16 << 20, transcendentals=0),
        compiler_params=pltpu.CompilerParams(vmem_limit_bytes=24 << 20),
        name="readout_last" if last else "readout",
    )(place, *args)


def after(value, *others):
    return lax.optimization_barrier((value, *others))[0]


def row_exchange(payload):
    return lax.all_to_all(payload, "x", 0, 0, tiled=True)


def to_row(*levels):
    return row_exchange(jnp.broadcast_to(jnp.stack(levels)[None], (4, len(levels)) + levels[0].shape))


def sent(payload):
    return [payload] + [xor_permute(payload, "x", d) for d in range(1, 4)]


def on_device(queries, keys, values, level_weights, out_gain):
    core, x, z, y = (lax.axis_index(a) for a in ("c", "x", "z", "y"))
    block = ((y * 8 + z) * 4 + x) * 2 + core
    place = jnp.stack([core, x, block]).astype(jnp.int32)
    level_rows = jnp.transpose(level_weights, (1, 2, 0))
    gain = out_gain.astype(F32).reshape(1, HEADS * DV)

    give = block_state(place, keys, values, 1)
    zero_own = xor_permute(give, "c", 1)
    keep = block_state(after(place, give), keys, values, 0)
    half = keep + zero_own
    u = row_exchange(half.reshape(4, GROUP, DV, DK))
    zero_oth = xor_permute(after(keep, half), "c", 1)
    local = local_attention(after(place, half), queries, keys, values, level_rows)
    u, local, zero_oth = lax.optimization_barrier((u, local, zero_oth))
    t3 = (u[0] + u[1]) + (u[2] + u[3])
    l3 = xor_permute(t3, "z", 1)
    l1 = xor_permute(after(half, u), "x", 1)
    t4 = t3 + l3
    l4 = xor_permute(t4, "z", 2)
    t5 = after(t4 + l4, l1)
    l2 = xor_permute(half + l1, "x", 3)
    l5 = xor_permute(t5, "z", 4)
    own34 = to_row(l3, l4)
    t6 = t5 + l5
    p1, p2, p3 = (xor_permute(t6, "y", d) for d in (1, 2, 3))
    own1 = l1.reshape(4, 1, GROUP, DV, DK)
    oth1 = xor_permute(own1, "c", 1)
    p1 = after(p1, l2, oth1)
    top = jnp.stack([l5, p1, p2 + p3])
    own567 = sent(top)
    own2 = after(l2, top).reshape(4, 1, GROUP, DV, DK)
    own = [zero_own.reshape(4, 1, GROUP, DV, DK), own1, own2]
    oth = [zero_oth.reshape(4, 1, GROUP, DV, DK), oth1, xor_permute(own2, "c", 1)]
    own34 = after(own34, top)
    own.append(own34)
    oth.append(xor_permute(own34, "c", 1))
    mid = readout(place, queries, local, level_rows, 0, own, oth, [False] * 4)
    own567 = jnp.stack([after(part, mid) for part in own567])
    oth567 = xor_permute(own567, "c", 1)
    return readout(place, queries, mid, level_rows, 5, [own567], [oth567], [True], gain=gain)


def solution(mesh):
    wide = Mesh(mesh.devices.reshape(4, 8, 4, 2), ("y", "z", "x", "c"))
    split = ("y", "z", "x", "c")
    return jax.shard_map(
        on_device,
        mesh=wide,
        in_specs=(P(split, None), P(split, None), P(split, None), P(split, None, None), P()),
        out_specs=P(split, None),
        check_vma=False,
    )
```

```python
import functools

import jax
import jax.numpy as jnp
from jax import lax
from jax.experimental import pallas as pl
from jax.experimental.pallas import tpu as pltpu
from jax.sharding import Mesh, PartitionSpec as P

HEADS = 32
DK = 128
DV = 64
TOK = 512
HALF = 256
TILE = 128
LOCAL = 10
LEVELS = 18
GROUP = 4
STEPS = HEADS // GROUP
SIDE = HEADS // 2
EPS = 1e-06
F32 = jnp.float32
BF16 = jnp.bfloat16


def xor_permute(value, axis, mask):
    size = lax.axis_size(axis)
    return lax.ppermute(value, axis, [(i, i ^ mask) for i in range(size)])


def dot(a, b):
    return jnp.dot(a, b, preferred_element_type=F32)


def dot_t0(a, b):
    return lax.dot_general(a, b, (((0,), (0,)), ((), ())), preferred_element_type=F32)


def dot_t1(a, b):
    return lax.dot_general(a, b, (((1,), (1,)), ((), ())), preferred_element_type=F32)


def state_kernel(other, place_ref, k_hbm, v_hbm, s_ref, k_buf, v_buf, k_sem, v_sem):
    side = place_ref[0] ^ other
    chunks = SIDE // GROUP

    def copies(i):
        at = side * chunks + i
        k_at = pl.ds(pl.multiple_of(at * GROUP * DK, GROUP * DK), GROUP * DK)
        v_at = pl.ds(pl.multiple_of(at * GROUP * DV, GROUP * DV), GROUP * DV)
        return (
            pltpu.make_async_copy(k_hbm.at[:, k_at], k_buf.at[i], k_sem.at[i]),
            pltpu.make_async_copy(v_hbm.at[:, v_at], v_buf.at[i], v_sem.at[i]),
        )

    for i in range(chunks):
        for copy in copies(i):
            copy.start()
    for i in range(chunks):
        for copy in copies(i):
            copy.wait()
        for pair in range(GROUP // 2):
            v = v_buf[i, :, pair * 2 * DV : (pair + 1) * 2 * DV]
            k = k_buf[i, :, pair * 2 * DK : (pair + 1) * 2 * DK]
            both = dot_t0(v, k)
            for j in range(2):
                s_ref[i * GROUP + 2 * pair + j] = both[j * DV : (j + 1) * DV, j * DK : (j + 1) * DK]


def block_state(place, keys, values, other):
    hbm = pl.BlockSpec(memory_space=pltpu.HBM)
    chunks = SIDE // GROUP
    return pl.pallas_call(
        functools.partial(state_kernel, other),
        in_specs=[pl.BlockSpec(memory_space=pltpu.SMEM), hbm, hbm],
        out_specs=pl.BlockSpec(memory_space=pltpu.VMEM),
        out_shape=jax.ShapeDtypeStruct((SIDE, DV, DK), F32),
        scratch_shapes=[
            pltpu.VMEM((chunks, TOK, GROUP * DK), BF16),
            pltpu.VMEM((chunks, TOK, GROUP * DV), BF16),
            pltpu.SemaphoreType.DMA((chunks,)),
            pltpu.SemaphoreType.DMA((chunks,)),
        ],
        cost_estimate=pl.CostEstimate(flops=1 << 28, bytes_accessed=4 << 20, transcendentals=0),
        compiler_params=pltpu.CompilerParams(vmem_limit_bytes=16 << 20),
        name="block_state",
    )(place, keys, values)


def diagonal_weight(rows):
    group = lax.broadcasted_iota(jnp.int32, (16, TILE), 0)
    lane = lax.broadcasted_iota(jnp.int32, (16, TILE), 1)
    other = lane >> 3
    xored = group ^ other
    coarse = jnp.zeros((16, TILE), F32)
    for level in range(4, 8):
        coarse = jnp.where((xored >> (level - 4)) == 1, rows[level], coarse)
    coarse = jnp.where(other > group, coarse, 0.0)
    sub = lax.broadcasted_iota(jnp.int32, (8, TILE), 0)
    low = lax.broadcasted_iota(jnp.int32, (8, TILE), 1)
    place = low & 7
    near = sub ^ place
    fine = jnp.broadcast_to(rows[0], (8, TILE))
    for level in range(1, 4):
        fine = jnp.where((near >> (level - 1)) == 1, rows[level], fine)
    fine = jnp.where(place >= sub, fine, 0.0)
    owner = low >> 3
    return jnp.concatenate(
        [
            jnp.where(owner == i, fine, jnp.broadcast_to(coarse[i : i + 1], (8, TILE)))
            for i in range(16)
        ],
        axis=0,
    )


def local_kernel(place_ref, q_ref, k_ref, v_ref, lw_ref, o_ref, w_ref):
    step = pl.program_id(0)

    for r in range(SIDE // GROUP):

        @pl.when(step % 4 == r)
        def _():
            w_ref[...] = lw_ref[:LOCAL, r * GROUP : (r + 1) * GROUP].astype(F32)

    def row(level, head, at, size):
        return w_ref[level, head : head + 1, at : at + size]

    v_t = [v_ref[:, p * 2 * DV : (p + 1) * 2 * DV].T for p in range(GROUP // 2)]
    parts = {}
    for head in range(GROUP):
        cols = slice(head * DK, (head + 1) * DK)
        v_head = v_t[head // 2][(head % 2) * DV : (head % 2 + 1) * DV]
        for block in range(2):
            at = block * HALF
            q = q_ref[at : at + HALF, cols]
            k = k_ref[at : at + HALF, cols]
            if block:
                first = dot(v_head[:, :HALF], k_ref[:HALF, cols]).astype(BF16)
                scores = dot_t1(jnp.concatenate([k, first], axis=0), q)
                extra = scores[HALF:] * row(9, head, at, HALF)
            else:
                scores = dot_t1(k, q)
                extra = None
            tiles = []
            for tile in range(2):
                part = slice(tile * TILE, (tile + 1) * TILE)
                rows = [row(l, head, at + tile * TILE, TILE) for l in range(8)]
                tiles.append((scores[part, part] * diagonal_weight(rows)).astype(BF16))
            upper = (scores[:TILE, TILE:HALF] * row(8, head, at + TILE, TILE)).astype(BF16)
            weighted = jnp.concatenate(
                [
                    jnp.concatenate([tiles[0], upper], axis=1),
                    jnp.concatenate([jnp.zeros((TILE, TILE), BF16), tiles[1]], axis=1),
                ],
                axis=0,
            )
            parts[head, block] = (v_head[:, at : at + HALF], weighted, extra)
    for (head, block), (v_part, weighted, extra) in parts.items():
        out = dot(v_part, weighted)
        out = out if extra is None else out + extra
        o_ref[head, :, block * HALF : (block + 1) * HALF] = out.astype(BF16)


def local_attention(place, queries, keys, values, level_rows):
    return pl.pallas_call(
        local_kernel,
        grid_spec=pltpu.PrefetchScalarGridSpec(
            num_scalar_prefetch=1,
            grid=(STEPS,),
            in_specs=[
                pl.BlockSpec((TOK, GROUP * DK), lambda i, p: (0, i)),
                pl.BlockSpec((TOK, GROUP * DK), lambda i, p: (0, i)),
                pl.BlockSpec((TOK, GROUP * DV), lambda i, p: (0, i)),
                pl.BlockSpec((LEVELS, SIDE, TOK), lambda i, p: (0, i // 4, 0)),
            ],
            out_specs=pl.BlockSpec((GROUP, DV, TOK), lambda i, p: (i, 0, 0)),
            scratch_shapes=[pltpu.VMEM((LOCAL, GROUP, TOK), F32)],
        ),
        out_shape=jax.ShapeDtypeStruct((HEADS, DV, TOK), BF16),
        cost_estimate=pl.CostEstimate(flops=8 << 30, bytes_accessed=16 << 20, transcendentals=0),
        compiler_params=pltpu.CompilerParams(vmem_limit_bytes=60 << 20),
        name="local_attention",
    )(place, queries, keys, values, level_rows)


def readout_kernel(base, counts, last, part, *refs):
    refs = list(refs)
    place_ref, q_ref, sum_ref, lw_ref = refs[:4]
    refs = refs[4:]
    gain_ref = refs.pop(0) if last else None
    if part == 1:
        refs.pop(0)
    per = 2 if part is None else 1
    sides = [refs[per * i : per * i + per] for i in range(len(counts))]
    o_ref, lhs_ref, w_ref = refs[-3:]
    step = pl.program_id(0)
    levels = sum(counts)

    for r in range(SIDE // GROUP):

        @pl.when(step % 4 == r)
        def _():
            for l in range(levels):
                flag = ((place_ref[2] >> (base + l)) & 1).astype(F32)
                rows = lw_ref[LOCAL + base + l, r * GROUP : (r + 1) * GROUP]
                w_ref[l] = rows.astype(F32) * flag

    def stage(which):
        at = 0
        for pair, count in zip(sides, counts):
            for level in range(count):
                for j in range(GROUP):
                    lhs_ref[j, at : at + DV] = pair[which][0, level, j].astype(BF16)
                at += DV

    if part is None:

        @pl.when(step < STEPS // 2)
        def _():
            stage(0)

        @pl.when(step >= STEPS // 2)
        def _():
            stage(1)

    else:
        stage(0)

    sums = {}
    for head in range(GROUP):
        for block in range(2):
            at = slice(block * HALF, (block + 1) * HALF)
            r = dot_t1(lhs_ref[head], q_ref[at, head * DK : (head + 1) * DK])
            acc = sum_ref[head, :, at].astype(F32)
            for l in range(levels):
                acc = acc + r[l * DV : (l + 1) * DV] * w_ref[l, head : head + 1, at]
            if last:
                mean = jnp.mean(acc * acc, axis=0, keepdims=True)
                sums[head, block] = acc * lax.rsqrt(mean + EPS)
            else:
                o_ref[head, :, at] = acc
    if last:
        for pair in range(GROUP // 2):
            cols = slice(pair * 2 * DV, (pair + 1) * 2 * DV)
            for block in range(2):
                flat = jnp.concatenate([sums[2 * pair, block], sums[2 * pair + 1, block]], axis=0).T
                at = slice(block * HALF, (block + 1) * HALF)
                o_ref[at, cols] = (flat * gain_ref[:, cols]).astype(BF16)


def readout(place, queries, total, level_rows, base, own, oth, distance, gain=None, part=None, prior=None):
    last = gain is not None
    counts = tuple(o.shape[1] for o in own)
    levels = sum(counts)

    def side(i, place):
        return place[0] ^ (i // 4 if part is None else part)

    def group(i, place):
        return 4 * side(i, place) + i % 4

    def pieces(array, second, by_distance):
        def index(i, place):
            at = i
            if part is None:
                at = jnp.maximum(i - 4, 0) if second else jnp.minimum(i, 3)
            return (at ^ place[1] if by_distance else at, 0, 0, 0, 0)

        return pl.BlockSpec((1,) + array.shape[1:], index)

    heads = pl.BlockSpec((GROUP, DV, TOK), lambda i, p: (group(i, p), 0, 0))
    flat = pl.BlockSpec((TOK, GROUP * DV), lambda i, p: (0, group(i, p)))
    args = [queries, total, level_rows]
    specs = [
        pl.BlockSpec((TOK, GROUP * DK), lambda i, p: (0, group(i, p))),
        heads,
        pl.BlockSpec((LEVELS, SIDE, TOK), lambda i, p: (0, side(i, p), 0)),
    ]
    if last:
        args.append(gain)
        specs.append(pl.BlockSpec((1, GROUP * DV), lambda i, p: (0, group(i, p))))
    aliases = {}
    if part == 1:
        aliases = {1 + len(args): 0}
        args.append(prior)
        specs.append(pl.BlockSpec(memory_space=pl.ANY))
    for mine, theirs, by_distance in zip(own, oth, distance):
        if part != 1:
            args.append(mine)
            specs.append(pieces(mine, False, by_distance))
        if part != 0:
            args.append(theirs)
            specs.append(pieces(theirs, True, by_distance))
    return pl.pallas_call(
        functools.partial(readout_kernel, base, counts, last, part),
        grid_spec=pltpu.PrefetchScalarGridSpec(
            num_scalar_prefetch=1,
            grid=(STEPS if part is None else STEPS // 2,),
            in_specs=specs,
            out_specs=flat if last else heads,
            scratch_shapes=[
                pltpu.VMEM((GROUP, levels * DV, DK), BF16),
                pltpu.VMEM((levels, GROUP, TOK), F32),
            ],
        ),
        out_shape=jax.ShapeDtypeStruct((TOK, HEADS * DV), BF16)
        if last
        else jax.ShapeDtypeStruct((HEADS, DV, TOK), F32),
        cost_estimate=pl.CostEstimate(flops=levels << 30, bytes_accessed=16 << 20, transcendentals=0),
        compiler_params=pltpu.CompilerParams(vmem_limit_bytes=24 << 20),
        input_output_aliases=aliases,
        name="readout_last" if last else "readout",
    )(place, *args)


def after(value, *others):
    return lax.optimization_barrier((value, *others))[0]


def row_exchange(payload):
    return lax.all_to_all(payload, "x", 0, 0, tiled=True)


def to_row(*levels):
    return row_exchange(jnp.broadcast_to(jnp.stack(levels)[None], (4, len(levels)) + levels[0].shape))


def sent(payload):
    return [payload] + [xor_permute(payload, "x", d) for d in range(1, 4)]


def on_device(queries, keys, values, level_weights, out_gain):
    core, x, z, y = (lax.axis_index(a) for a in ("c", "x", "z", "y"))
    block = ((y * 8 + z) * 4 + x) * 2 + core
    place = jnp.stack([core, x, block]).astype(jnp.int32)
    level_rows = jnp.transpose(level_weights, (1, 2, 0))
    gain = out_gain.astype(F32).reshape(1, HEADS * DV)

    give = block_state(place, keys, values, 1)
    zero_own = xor_permute(give, "c", 1)
    keep = block_state(after(place, give), keys, values, 0)
    half = keep + zero_own
    u = row_exchange(half.reshape(4, GROUP, DV, DK))
    zero_oth = xor_permute(after(keep, half), "c", 1)
    local = local_attention(after(place, half), queries, keys, values, level_rows)
    u, local, zero_oth = lax.optimization_barrier((u, local, zero_oth))
    t3 = (u[0] + u[1]) + (u[2] + u[3])
    l3 = xor_permute(t3, "z", 1)
    l1 = xor_permute(after(half, u), "x", 1)
    t4 = t3 + l3
    l4 = xor_permute(t4, "z", 2)
    t5 = after(t4 + l4, l1)
    l2 = xor_permute(half + l1, "x", 3)
    l5 = xor_permute(t5, "z", 4)
    own34 = to_row(l3, l4)
    t6 = t5 + l5
    p1, p2, p3 = (xor_permute(t6, "y", d) for d in (1, 2, 3))
    own1 = l1.reshape(4, 1, GROUP, DV, DK)
    oth1 = xor_permute(own1, "c", 1)
    p1 = after(p1, l2, oth1)
    top = jnp.stack([l5, p1, p2 + p3])
    own567 = sent(top)
    own2 = after(l2, top).reshape(4, 1, GROUP, DV, DK)
    own = [zero_own.reshape(4, 1, GROUP, DV, DK), own1, own2]
    oth = [zero_oth.reshape(4, 1, GROUP, DV, DK), oth1, xor_permute(own2, "c", 1)]
    own34 = after(own34, top)
    own.append(own34)
    oth.append(xor_permute(own34, "c", 1))
    mid = readout(place, queries, local, level_rows, 0, own, oth, [False] * 4)
    own567 = jnp.stack([after(part, mid) for part in own567])
    oth567 = xor_permute(own567, "c", 1)
    half_done = readout(
        place, queries, mid, level_rows, 5, [own567], [oth567], [True], gain=gain, part=0
    )
    return readout(
        place, queries, mid, level_rows, 5, [own567], [oth567], [True], gain=gain, part=1, prior=half_done
    )


def solution(mesh):
    wide = Mesh(mesh.devices.reshape(4, 8, 4, 2), ("y", "z", "x", "c"))
    split = ("y", "z", "x", "c")
    return jax.shard_map(
        on_device,
        mesh=wide,
        in_specs=(P(split, None), P(split, None), P(split, None), P(split, None, None), P()),
        out_specs=P(split, None),
        check_vma=False,
    )
```

```python
import functools

import jax
import jax.numpy as jnp
from jax import lax
from jax.experimental import pallas as pl
from jax.experimental.pallas import tpu as pltpu
from jax.sharding import Mesh, PartitionSpec as P

HEADS = 32
DK = 128
DV = 64
TOK = 512
HALF = 256
TILE = 128
LOCAL = 10
LEVELS = 18
GROUP = 4
STEPS = HEADS // GROUP
SIDE = HEADS // 2
EPS = 1e-06
F32 = jnp.float32
BF16 = jnp.bfloat16


def xor_permute(value, axis, mask):
    size = lax.axis_size(axis)
    return lax.ppermute(value, axis, [(i, i ^ mask) for i in range(size)])


def dot(a, b):
    return jnp.dot(a, b, preferred_element_type=F32)


def dot_t0(a, b):
    return lax.dot_general(a, b, (((0,), (0,)), ((), ())), preferred_element_type=F32)


def dot_t1(a, b):
    return lax.dot_general(a, b, (((1,), (1,)), ((), ())), preferred_element_type=F32)


def state_kernel(other, place_ref, k_hbm, v_hbm, s_ref, k_buf, v_buf, k_sem, v_sem):
    side = place_ref[0] ^ other
    chunks = SIDE // GROUP

    def copies(i):
        at = side * chunks + i
        k_at = pl.ds(pl.multiple_of(at * GROUP * DK, GROUP * DK), GROUP * DK)
        v_at = pl.ds(pl.multiple_of(at * GROUP * DV, GROUP * DV), GROUP * DV)
        return (
            pltpu.make_async_copy(k_hbm.at[:, k_at], k_buf.at[i], k_sem.at[i]),
            pltpu.make_async_copy(v_hbm.at[:, v_at], v_buf.at[i], v_sem.at[i]),
        )

    for i in range(chunks):
        for copy in copies(i):
            copy.start()
    for i in range(chunks):
        for copy in copies(i):
            copy.wait()
        for pair in range(GROUP // 2):
            v = v_buf[i, :, pair * 2 * DV : (pair + 1) * 2 * DV]
            k = k_buf[i, :, pair * 2 * DK : (pair + 1) * 2 * DK]
            both = dot_t0(v, k)
            for j in range(2):
                s_ref[i * GROUP + 2 * pair + j] = both[j * DV : (j + 1) * DV, j * DK : (j + 1) * DK]


def block_state(place, keys, values, other):
    hbm = pl.BlockSpec(memory_space=pltpu.HBM)
    chunks = SIDE // GROUP
    return pl.pallas_call(
        functools.partial(state_kernel, other),
        in_specs=[pl.BlockSpec(memory_space=pltpu.SMEM), hbm, hbm],
        out_specs=pl.BlockSpec(memory_space=pltpu.VMEM),
        out_shape=jax.ShapeDtypeStruct((SIDE, DV, DK), F32),
        scratch_shapes=[
            pltpu.VMEM((chunks, TOK, GROUP * DK), BF16),
            pltpu.VMEM((chunks, TOK, GROUP * DV), BF16),
            pltpu.SemaphoreType.DMA((chunks,)),
            pltpu.SemaphoreType.DMA((chunks,)),
        ],
        cost_estimate=pl.CostEstimate(flops=1 << 28, bytes_accessed=4 << 20, transcendentals=0),
        compiler_params=pltpu.CompilerParams(vmem_limit_bytes=16 << 20),
        name="block_state",
    )(place, keys, values)


def diagonal_weight(rows):
    group = lax.broadcasted_iota(jnp.int32, (16, TILE), 0)
    lane = lax.broadcasted_iota(jnp.int32, (16, TILE), 1)
    other = lane >> 3
    xored = group ^ other
    coarse = jnp.zeros((16, TILE), F32)
    for level in range(4, 8):
        coarse = jnp.where((xored >> (level - 4)) == 1, rows[level], coarse)
    coarse = jnp.where(other > group, coarse, 0.0)
    sub = lax.broadcasted_iota(jnp.int32, (8, TILE), 0)
    low = lax.broadcasted_iota(jnp.int32, (8, TILE), 1)
    place = low & 7
    near = sub ^ place
    fine = jnp.broadcast_to(rows[0], (8, TILE))
    for level in range(1, 4):
        fine = jnp.where((near >> (level - 1)) == 1, rows[level], fine)
    fine = jnp.where(place >= sub, fine, 0.0)
    owner = low >> 3
    return jnp.concatenate(
        [
            jnp.where(owner == i, fine, jnp.broadcast_to(coarse[i : i + 1], (8, TILE)))
            for i in range(16)
        ],
        axis=0,
    )


def local_kernel(place_ref, q_ref, k_ref, v_ref, lw_ref, o_ref, w_ref):
    step = pl.program_id(0)

    for r in range(SIDE // GROUP):

        @pl.when(step % 4 == r)
        def _():
            w_ref[...] = lw_ref[:, r * GROUP : (r + 1) * GROUP].astype(F32)

    def row(level, head, at, size):
        return w_ref[level, head : head + 1, at : at + size]

    v_t = [v_ref[:, p * 2 * DV : (p + 1) * 2 * DV].T for p in range(GROUP // 2)]
    parts = {}
    for head in range(GROUP):
        cols = slice(head * DK, (head + 1) * DK)
        v_head = v_t[head // 2][(head % 2) * DV : (head % 2 + 1) * DV]
        for block in range(2):
            at = block * HALF
            q = q_ref[at : at + HALF, cols]
            k = k_ref[at : at + HALF, cols]
            if block:
                first = dot(v_head[:, :HALF], k_ref[:HALF, cols]).astype(BF16)
                scores = dot_t1(jnp.concatenate([k, first], axis=0), q)
                extra = scores[HALF:] * row(9, head, at, HALF)
            else:
                scores = dot_t1(k, q)
                extra = None
            tiles = []
            for tile in range(2):
                part = slice(tile * TILE, (tile + 1) * TILE)
                rows = [row(l, head, at + tile * TILE, TILE) for l in range(8)]
                tiles.append((scores[part, part] * diagonal_weight(rows)).astype(BF16))
            upper = (scores[:TILE, TILE:HALF] * row(8, head, at + TILE, TILE)).astype(BF16)
            weighted = jnp.concatenate(
                [
                    jnp.concatenate([tiles[0], upper], axis=1),
                    jnp.concatenate([jnp.zeros((TILE, TILE), BF16), tiles[1]], axis=1),
                ],
                axis=0,
            )
            parts[head, block] = (v_head[:, at : at + HALF], weighted, extra)
    for (head, block), (v_part, weighted, extra) in parts.items():
        out = dot(v_part, weighted)
        out = out if extra is None else out + extra
        o_ref[head, :, block * HALF : (block + 1) * HALF] = out.astype(BF16)


def local_attention(place, queries, keys, values, level_rows):
    return pl.pallas_call(
        local_kernel,
        grid_spec=pltpu.PrefetchScalarGridSpec(
            num_scalar_prefetch=1,
            grid=(STEPS,),
            in_specs=[
                pl.BlockSpec((TOK, GROUP * DK), lambda i, p: (0, i)),
                pl.BlockSpec((TOK, GROUP * DK), lambda i, p: (0, i)),
                pl.BlockSpec((TOK, GROUP * DV), lambda i, p: (0, i)),
                pl.BlockSpec((LOCAL, SIDE, TOK), lambda i, p: (0, i // 4, 0)),
            ],
            out_specs=pl.BlockSpec((GROUP, DV, TOK), lambda i, p: (i, 0, 0)),
            scratch_shapes=[pltpu.VMEM((LOCAL, GROUP, TOK), F32)],
        ),
        out_shape=jax.ShapeDtypeStruct((HEADS, DV, TOK), BF16),
        cost_estimate=pl.CostEstimate(flops=8 << 30, bytes_accessed=16 << 20, transcendentals=0),
        compiler_params=pltpu.CompilerParams(vmem_limit_bytes=60 << 20),
        name="local_attention",
    )(place, queries, keys, values, level_rows)


def readout_kernel(base, counts, last, part, *refs):
    refs = list(refs)
    place_ref, q_ref, sum_ref, lw_ref = refs[:4]
    refs = refs[4:]
    gain_ref = refs.pop(0) if last else None
    if part == 1:
        refs.pop(0)
    per = 2 if part is None else 1
    sides = [refs[per * i : per * i + per] for i in range(len(counts))]
    o_ref, lhs_ref, w_ref = refs[-3:]
    step = pl.program_id(0)
    levels = sum(counts)

    for r in range(SIDE // GROUP):

        @pl.when(step % 4 == r)
        def _():
            for l in range(levels):
                flag = ((place_ref[2] >> (base + l)) & 1).astype(F32)
                rows = lw_ref[LOCAL + base + l, r * GROUP : (r + 1) * GROUP]
                w_ref[l] = rows.astype(F32) * flag

    def stage(which):
        at = 0
        for pair, count in zip(sides, counts):
            for level in range(count):
                for j in range(GROUP):
                    lhs_ref[j, at : at + DV] = pair[which][0, level, j].astype(BF16)
                at += DV

    if part is None:

        @pl.when(step < STEPS // 2)
        def _():
            stage(0)

        @pl.when(step >= STEPS // 2)
        def _():
            stage(1)

    else:
        stage(0)

    sums = {}
    for head in range(GROUP):
        for block in range(2):
            at = slice(block * HALF, (block + 1) * HALF)
            r = dot_t1(lhs_ref[head], q_ref[at, head * DK : (head + 1) * DK])
            acc = sum_ref[head, :, at].astype(F32)
            for l in range(levels):
                acc = acc + r[l * DV : (l + 1) * DV] * w_ref[l, head : head + 1, at]
            if last:
                mean = jnp.mean(acc * acc, axis=0, keepdims=True)
                sums[head, block] = acc * lax.rsqrt(mean + EPS)
            else:
                o_ref[head, :, at] = acc
    if last:
        for pair in range(GROUP // 2):
            cols = slice(pair * 2 * DV, (pair + 1) * 2 * DV)
            for block in range(2):
                flat = jnp.concatenate([sums[2 * pair, block], sums[2 * pair + 1, block]], axis=0).T
                at = slice(block * HALF, (block + 1) * HALF)
                o_ref[at, cols] = (flat * gain_ref[:, cols]).astype(BF16)


def readout(place, queries, total, level_rows, base, own, oth, distance, gain=None, part=None, prior=None):
    last = gain is not None
    counts = tuple(o.shape[1] for o in own)
    levels = sum(counts)

    def side(i, place):
        return place[0] ^ (i // 4 if part is None else part)

    def group(i, place):
        return 4 * side(i, place) + i % 4

    def pieces(array, second, by_distance):
        def index(i, place):
            at = i
            if part is None:
                at = jnp.maximum(i - 4, 0) if second else jnp.minimum(i, 3)
            return (at ^ place[1] if by_distance else at, 0, 0, 0, 0)

        return pl.BlockSpec((1,) + array.shape[1:], index)

    heads = pl.BlockSpec((GROUP, DV, TOK), lambda i, p: (group(i, p), 0, 0))
    flat = pl.BlockSpec((TOK, GROUP * DV), lambda i, p: (0, group(i, p)))
    args = [queries, total, level_rows]
    specs = [
        pl.BlockSpec((TOK, GROUP * DK), lambda i, p: (0, group(i, p))),
        heads,
        pl.BlockSpec((LEVELS, SIDE, TOK), lambda i, p: (0, side(i, p), 0)),
    ]
    if last:
        args.append(gain)
        specs.append(pl.BlockSpec((1, GROUP * DV), lambda i, p: (0, group(i, p))))
    aliases = {}
    if part == 1:
        aliases = {1 + len(args): 0}
        args.append(prior)
        specs.append(pl.BlockSpec(memory_space=pl.ANY))
    for mine, theirs, by_distance in zip(own, oth, distance):
        if part != 1:
            args.append(mine)
            specs.append(pieces(mine, False, by_distance))
        if part != 0:
            args.append(theirs)
            specs.append(pieces(theirs, True, by_distance))
    return pl.pallas_call(
        functools.partial(readout_kernel, base, counts, last, part),
        grid_spec=pltpu.PrefetchScalarGridSpec(
            num_scalar_prefetch=1,
            grid=(STEPS if part is None else STEPS // 2,),
            in_specs=specs,
            out_specs=flat if last else heads,
            scratch_shapes=[
                pltpu.VMEM((GROUP, levels * DV, DK), BF16),
                pltpu.VMEM((levels, GROUP, TOK), F32),
            ],
        ),
        out_shape=jax.ShapeDtypeStruct((TOK, HEADS * DV), BF16)
        if last
        else jax.ShapeDtypeStruct((HEADS, DV, TOK), F32),
        cost_estimate=pl.CostEstimate(flops=levels << 30, bytes_accessed=16 << 20, transcendentals=0),
        compiler_params=pltpu.CompilerParams(vmem_limit_bytes=24 << 20),
        input_output_aliases=aliases,
        name="readout_last" if last else "readout",
    )(place, *args)


def after(value, *others):
    return lax.optimization_barrier((value, *others))[0]


def row_exchange(payload):
    return lax.all_to_all(payload, "x", 0, 0, tiled=True)


def to_row(*levels):
    return row_exchange(jnp.broadcast_to(jnp.stack(levels)[None], (4, len(levels)) + levels[0].shape))


def sent(payload):
    return [payload] + [xor_permute(payload, "x", d) for d in range(1, 4)]


def on_device(queries, keys, values, level_weights, out_gain):
    core, x, z, y = (lax.axis_index(a) for a in ("c", "x", "z", "y"))
    block = ((y * 8 + z) * 4 + x) * 2 + core
    place = jnp.stack([core, x, block]).astype(jnp.int32)
    level_rows = jnp.transpose(level_weights, (1, 2, 0))
    gain = out_gain.astype(F32).reshape(1, HEADS * DV)

    give = block_state(place, keys, values, 1)
    zero_own = xor_permute(give, "c", 1)
    keep = block_state(after(place, give), keys, values, 0)
    half = keep + zero_own
    u = row_exchange(half.reshape(4, GROUP, DV, DK))
    zero_oth = xor_permute(after(keep, half), "c", 1)
    local = local_attention(after(place, half), queries, keys, values, level_rows)
    u, local, zero_oth = lax.optimization_barrier((u, local, zero_oth))
    t3 = (u[0] + u[1]) + (u[2] + u[3])
    l3 = xor_permute(t3, "z", 1)
    l1 = xor_permute(after(half, u), "x", 1)
    t4 = t3 + l3
    l4 = xor_permute(t4, "z", 2)
    t5 = after(t4 + l4, l1)
    l2 = xor_permute(half + l1, "x", 3)
    l5 = xor_permute(t5, "z", 4)
    own34 = to_row(l3, l4)
    t6 = t5 + l5
    p1, p2, p3 = (xor_permute(t6, "y", d) for d in (1, 2, 3))
    own1 = l1.reshape(4, 1, GROUP, DV, DK)
    oth1 = xor_permute(own1, "c", 1)
    p1 = after(p1, l2, oth1)
    top = jnp.stack([l5, p1, p2 + p3])
    own567 = sent(top)
    own2 = after(l2, top).reshape(4, 1, GROUP, DV, DK)
    own = [zero_own.reshape(4, 1, GROUP, DV, DK), own1, own2]
    oth = [zero_oth.reshape(4, 1, GROUP, DV, DK), oth1, xor_permute(own2, "c", 1)]
    own34 = after(own34, top)
    own.append(own34)
    oth.append(xor_permute(own34, "c", 1))
    mid = readout(place, queries, local, level_rows, 0, own, oth, [False] * 4)
    own567 = jnp.stack([after(part, mid) for part in own567])
    oth567 = xor_permute(own567, "c", 1)
    half_done = readout(
        place, queries, mid, level_rows, 5, [own567], [oth567], [True], gain=gain, part=0
    )
    return readout(
        place, queries, mid, level_rows, 5, [own567], [oth567], [True], gain=gain, part=1, prior=half_done
    )


def solution(mesh):
    wide = Mesh(mesh.devices.reshape(4, 8, 4, 2), ("y", "z", "x", "c"))
    split = ("y", "z", "x", "c")
    return jax.shard_map(
        on_device,
        mesh=wide,
        in_specs=(P(split, None), P(split, None), P(split, None), P(split, None, None), P()),
        out_specs=P(split, None),
        check_vma=False,
    )
```
